32 devices in a mesh: prow: 4 (over z), pcol: 8 (over y, x, core).
Axes of the slice: x: 2, y: 2, z: 4, core: 2. Of those that a mesh axis runs over, the one named last changes fastest.
Arguments:
- blocks: bfloat16 [2048, 64, 128], P(('prow', 'pcol')), may hold values from -6 to 6
- owner: int32 [2048, 1], P(('prow', 'pcol')), may hold values from 0 to 31; in each aligned block of 64 rows (0 to 63, 64 to 127, ...) at most 2 rows name the same one
- row_offset: int32 [2048], P(('prow', 'pcol')), may hold values from 0 to 320
- col_offset: int32 [2048], P(('prow', 'pcol')), may hold values from 0 to 256
- exposure: int32 [2048], P(('prow', 'pcol')), may hold values from 0 to 255
- basis_rows: bfloat16 [21, 31], replicated, may hold values from -1 to 1
- basis_cols: bfloat16 [21, 31], replicated, may hold values from -1 to 1
- coef_table: float32 [256, 21], replicated, may hold values from -1.25 to 1.25
- weight_table: float32 [256], replicated, may hold values from 0.2 to 2
- det_taps: float32 [31], replicated, may hold values from 0.02 to 0.12
Outputs:
- coadd: float32 [1536, 3072], P('prow', 'pcol')
- detection: float32 [1536, 3072], P('prow', 'pcol')
The draws below stay inside these ranges and needn't reach their ends.
Inputs may be any that keep to these rules, and one draw needn't show every extreme that they name: The blocks of one device name one owner at most 2 times; some device names some owner exactly 2 times.
All inputs are finite; a program needn't handle non-finite values.
Results may differ from the reference program's by a relative error of at most 0.009.
Values may be sent and summed in bfloat16 or wider, within the bound.
A program may use at most 192 MiB of HBM per device.

```python
import math
import jax
import jax.numpy as jnp
import numpy as np
from jax import lax

BASIS = 21
TAPS = 31
DET_R = 15
BH = 64
BW = 128
PATCH = 384
NB = 64
CAP = 2
NTAB = 256
NDEV = 32
TOTAL_BLOCKS = 2048
NX = 1536
NY = 3072
N_PCOL = 8


def plant(values, key, smallest, top_value):
    index_at = [jax.random.randint(jax.random.fold_in(key, axis), (), 0, length) for axis, length in enumerate(values.shape)]
    longest = values.shape.index(max(values.shape))
    beside = index_at[:longest] + [(index_at[longest] + 1) % values.shape[longest]] + index_at[longest + 1:]
    return values.at[tuple(index_at)].set(smallest).at[tuple(beside)].set(top_value)


def block_levels(own_key, shape, cuts, least, top_value):
    def one(dim, parts):
        steps = jax.random.uniform(jax.random.fold_in(jax.random.fold_in(own_key, 6), dim), (parts,), jnp.float32, least / len(cuts), top_value / len(cuts))
        return jnp.repeat(jnp.exp(steps), shape[dim] // parts).reshape((-1,) + (1,) * (len(shape) - dim - 1))

    level = one(*cuts[0])
    for cut in cuts[1:]:
        level = level * one(*cut)
    return level


def shared_out(stream_key, own, number, rows, count, top, most, skew):
    ranking = jax.random.permutation(stream_key, count)
    crowded, common = shares(count, rows * top, most, skew, True), shares(count, rows * top, most, skew, False)
    places = jnp.arange(count)

    def named(lengths, turn):
        used = int((lengths > 0).sum())
        fixed = max(1, used // 4)
        moved = fixed + (places - fixed + turn * (used - fixed)) % max(1, count - fixed)
        return jnp.zeros((count,), jnp.int32).at[ranking[jnp.where(places < fixed, places, moved)]].set(jnp.asarray(lengths, jnp.int32))

    lengths = jnp.where(number % 4 == 0, named(crowded, number // 4), named(common, number - number // 4 - 1))
    mixed = jax.random.permutation(jax.random.fold_in(own, 3), count)
    donor, sink = mixed[0:count // 2 * 2:2], mixed[1:count // 2 * 2:2]
    margin = jnp.minimum(lengths[donor] - 1, most - lengths[sink]) // 2
    margin = jnp.where((donor == ranking[0]) | (sink == ranking[0]) | (lengths[sink] == 0), 0, jnp.maximum(margin, 0))
    moved = jax.random.randint(jax.random.fold_in(own, 4), (count // 2,), 0, 1 << 20) % (margin + 1)
    lengths = lengths.at[donor].add(-moved).at[sink].add(moved)
    labels = jnp.searchsorted(jnp.cumsum(lengths), jnp.arange(rows * top), side="right").astype(jnp.int32)
    table = labels.reshape(top, rows).T
    table = table[jax.random.permutation(jax.random.fold_in(own, 1), rows)]
    turn = jax.random.randint(jax.random.fold_in(own, 2), (rows, 1), 0, top)
    return jnp.take_along_axis(table, (jnp.arange(top)[None, :] + turn) % top, axis=1)


def shares(number_of, total, bound, skew, full):
    loads = [(1 << 20) // math.isqrt(grade ** skew) + 1 for grade in range(1, number_of + 1)]
    largest = bound if full else min(bound, max(-(-total // number_of), total * loads[0] // sum(loads)))
    least = 1 if total - largest >= number_of - 1 else 0
    counts, spare = [largest] + [least] * (number_of - 1), total - largest - least * (number_of - 1)
    while spare > 0:
        candidates = [i for i in range(1, number_of) if counts[i] < largest] or [i for i in range(1, number_of) if counts[i] < bound]
        pool, left = sum([loads[i] for i in candidates]), spare
        for i in candidates:
            more = min(bound - counts[i], max(1, left * loads[i] // pool), spare)
            counts[i] = counts[i] + more
            spare = spare - more
    return np.array(counts)


def noise(key, extent, deviation, most, pieces=(), dtype=jnp.bfloat16):
    gain = block_levels(key, extent, pieces, -0.22, 0.18) if pieces else 1.0
    result = jax.random.normal(key, extent, jnp.float32) * deviation * gain
    return jnp.minimum(jnp.maximum(result, -most), most).astype(dtype)


def setup_inputs(seed: int = 0) -> dict:
    streams_of = jax.random.split(jax.random.key(seed), 11)
    blocks = noise(streams_of[0], (TOTAL_BLOCKS, BH, BW), 1.0, 6.0, ((0, 32),))
    owner_keys = jax.random.split(jax.random.fold_in(streams_of[1], 1), TOTAL_BLOCKS // NB)
    owner_turns = jax.random.permutation(jax.random.fold_in(streams_of[1], 3), TOTAL_BLOCKS // NB)
    owner = jax.vmap(lambda own, number: shared_out(jax.random.fold_in(streams_of[1], 2), own, number, NB, NDEV, 1, CAP, 2))(owner_keys, owner_turns).reshape((TOTAL_BLOCKS, 1))
    row_offset = plant(jax.random.randint(streams_of[2], (TOTAL_BLOCKS,), 0, PATCH - BH + 1), jax.random.fold_in(streams_of[2], 1), 0, PATCH - BH).astype(jnp.int32)
    col_offset = plant(jax.random.randint(streams_of[3], (TOTAL_BLOCKS,), 0, PATCH - BW + 1), jax.random.fold_in(streams_of[3], 1), 0, PATCH - BW).astype(jnp.int32)
    exposure = plant(jax.random.randint(streams_of[4], (TOTAL_BLOCKS,), 0, NTAB), jax.random.fold_in(streams_of[4], 1), 0, NTAB - 1).astype(jnp.int32)
    basis_rows = noise(streams_of[5], (BASIS, TAPS), TAPS ** -0.5, 1.0)
    basis_cols = noise(streams_of[6], (BASIS, TAPS), TAPS ** -0.5, 1.0)
    coef_table = noise(streams_of[7], (NTAB, BASIS), BASIS ** -0.5, 1.25, (), jnp.float32)
    weight_table = jnp.clip(jnp.exp(jax.random.uniform(streams_of[8], (NTAB,), jnp.float32, math.log(0.2), math.log(2.0))), 0.2, 2.0)
    det_taps = jnp.clip(jax.random.uniform(streams_of[9], (2 * DET_R + 1,), jnp.float32, 0.02, 0.12), 0.02, 0.12)
    return dict(blocks=blocks, owner=owner, row_offset=row_offset, col_offset=col_offset, exposure=exposure, basis_rows=basis_rows, basis_cols=basis_cols, coef_table=coef_table, weight_table=weight_table, det_taps=det_taps)


def match_group(pixels, coefs, basis_rows, basis_cols):
    half = TAPS // 2
    taps = jnp.arange(TAPS)
    cols_in = jnp.arange(BW)
    rows_in = jnp.arange(BH)
    col_hits = ((cols_in[:, None, None] - cols_in[None, :, None] + half) == taps[None, None, :]).astype(jnp.float32)
    col_table = jnp.einsum('bct,kt->bkc', col_hits, basis_cols.astype(jnp.float32))
    section = jnp.einsum('gab,bkc->gakc', pixels.astype(jnp.float32), col_table).astype(jnp.bfloat16)
    scaled = (coefs[:, :, None] * basis_rows.astype(jnp.float32)[None]).astype(jnp.bfloat16)
    row_hits = ((rows_in[None, :, None] - rows_in[:, None, None] + half) == taps[None, None, :]).astype(jnp.float32)
    row_table = jnp.einsum('rat,gkt->grka', row_hits, scaled.astype(jnp.float32))
    return jnp.einsum('grka,gakc->grc', row_table, section.astype(jnp.float32)).astype(jnp.bfloat16)


def reference(blocks, owner, row_offset, col_offset, exposure, basis_rows, basis_cols, coef_table, weight_table, det_taps):
    group = 64
    count = blocks.shape[0]
    while count % group != 0:
        group = group // 2
    coefs = coef_table[exposure]
    weights = weight_table[exposure].astype(jnp.bfloat16).astype(jnp.float32)

    def one(args):
        pixels, coef, weight = args
        matched = match_group(pixels, coef, basis_rows, basis_cols)
        return (weight[:, None, None] * matched.astype(jnp.float32)).astype(jnp.bfloat16)

    weighted = lax.map(one, (blocks.reshape(count // group, group, BH, BW), coefs.reshape(count // group, group, BASIS), weights.reshape(count // group, group)))
    weighted = weighted.reshape(count, BH, BW)
    dest = owner[:, 0].astype(jnp.int32)
    top_rows = ((dest // N_PCOL) * PATCH + row_offset).astype(jnp.int32)
    left_cols = ((dest % N_PCOL) * PATCH + col_offset).astype(jnp.int32)

    def place(index, carry):
        total, depth = carry
        here_row = top_rows[index]
        here_col = left_cols[index]
        old = lax.dynamic_slice(total, (here_row, here_col), (BH, BW))
        total = lax.dynamic_update_slice(total, old + weighted[index].astype(jnp.float32), (here_row, here_col))
        old_depth = lax.dynamic_slice(depth, (here_row, here_col), (BH, BW))
        depth = lax.dynamic_update_slice(depth, old_depth + weights[index], (here_row, here_col))
        return (total, depth)

    start = (jnp.zeros((NX, NY), jnp.float32), jnp.zeros((NX, NY), jnp.float32))
    total, depth = lax.fori_loop(0, count, place, start)
    coadd = total / jnp.maximum(depth, 1.0)
    padded = jnp.pad(coadd, DET_R)
    across = jnp.zeros((NX, NY + 2 * DET_R), jnp.float32)
    for step in range(2 * DET_R + 1):
        across = across + det_taps[step] * padded[step:step + NX, :]
    detection = jnp.zeros((NX, NY), jnp.float32)
    for step in range(2 * DET_R + 1):
        detection = detection + det_taps[step] * across[:, step:step + NY]
    return coadd, detection
```

```python
import functools

import jax
import jax.numpy as jnp
from jax import lax
from jax.experimental import pallas as pl
from jax.experimental.pallas import tpu as pltpu
from jax.sharding import PartitionSpec as P

DET_R = 15
PATCH = 384
CAP = 2
LANES = 128
MESH = pl.DeviceIdType.MESH
EXACT = lax.Precision.HIGHEST


def padded_2(value, sides, width):
    for axis, dim in sides:
        size, length = (lax.axis_size(axis), value.shape[dim])
        up = [(i, (i + 1) % size) for i in range(size - 1)]
        down = [(j, i) for i, j in up]
        last = lax.slice_in_dim(value, length - width, length, axis=dim)
        leading = lax.slice_in_dim(value, 0, width, axis=dim)
        before = lax.ppermute(last, axis, up)
        after = lax.ppermute(leading, axis, down)
        value = jnp.concatenate([before, value, after], axis=dim)
    return value


def tables_kernel(
    kinds,
    slots,
    owner_col,
    owner_row,
    feats,
    exposure_col,
    table,
    col_src,
    row_src,
    info_out,
    coef_out,
    col_out,
    row_out,
):
    count = owner_col.shape[0]
    entries = table.shape[0]
    at_sub = lax.broadcasted_iota(jnp.int32, (count, count), 0)
    at_lane = lax.broadcasted_iota(jnp.int32, (count, count), 1)
    same = (owner_col[...] == owner_row[...]) & (at_sub < at_lane)
    rank = jnp.sum(same.astype(jnp.int32), axis=0, keepdims=True)
    slot = owner_row[...] * CAP + rank
    pick = (lax.broadcasted_iota(jnp.int32, (slots, count), 0) == slot).astype(jnp.float32)
    hits = (
        exposure_col[...] == lax.broadcasted_iota(jnp.int32, (count, entries), 1)
    ).astype(jnp.float32)
    found = jnp.dot(hits, table[...], precision=EXACT, preferred_element_type=jnp.float32)
    lane = lax.broadcasted_iota(jnp.int32, (count, LANES), 1)
    rounded = found.astype(jnp.bfloat16).astype(jnp.float32)
    found = jnp.where(lane == kinds, rounded, found)
    merged = jnp.where(lane <= kinds, found, feats[...])
    info = jnp.dot(pick, merged, precision=EXACT, preferred_element_type=jnp.float32)
    info_out[...] = info
    width = coef_out.shape[1]
    half = width // (kinds + 1)
    spread = (
        lax.broadcasted_iota(jnp.int32, (LANES, width), 0)
        == lax.broadcasted_iota(jnp.int32, (LANES, width), 1) // half
    ).astype(jnp.float32)
    coef_out[...] = jnp.dot(info, spread, precision=EXACT, preferred_element_type=jnp.float32)
    cols = col_out.shape[0]
    down = lax.broadcasted_iota(jnp.int32, (cols, LANES), 0)
    over = lax.broadcasted_iota(jnp.int32, (cols, LANES), 1)
    near = jnp.abs(over - down) <= DET_R
    for k in range(kinds):
        source = jnp.broadcast_to(col_src[k : k + 1, :], (cols, LANES))
        rolled = pltpu.roll(source, 0, 1, stride=1, stride_axis=0)
        col_out[:, k * LANES : (k + 1) * LANES] = jnp.where(near, rolled, 0.0).astype(jnp.bfloat16)
    rows = row_out.shape[0]
    down = lax.broadcasted_iota(jnp.int32, (rows, LANES), 0)
    over = lax.broadcasted_iota(jnp.int32, (rows, LANES), 1) % rows
    near = jnp.abs(over - down) <= DET_R
    for k in range(row_src.shape[0]):
        source = jnp.broadcast_to(row_src[k : k + 1, :], (rows, LANES))
        rolled = pltpu.roll(source, 0, 1, stride=1, stride_axis=0)
        row_out[:, k * LANES : (k + 1) * LANES] = jnp.where(near, rolled, 0.0)


def route_kernel(
    owners,
    ncol,
    kinds,
    picks,
    blocks,
    coefs,
    info,
    col_table,
    row_table,
    pixels_out,
    info_out,
    outgoing,
    sems,
):
    me = lax.axis_index("prow") * ncol + lax.axis_index("pcol")
    rows, cols = blocks.shape[1:]
    barrier = pltpu.get_barrier_semaphore()

    def place(device):
        return (device // ncol, device % ncol)

    def greet(i, carry):
        other = lax.rem(me + i, owners)
        pl.semaphore_signal(barrier, inc=1, device_id=place(other), device_id_type=MESH)
        return carry

    lax.fori_loop(1, owners, greet, 0)
    pl.semaphore_wait(barrier, owners - 1)

    def tell(i, carry):
        other = lax.rem(me + i, owners)
        pltpu.make_async_remote_copy(
            src_ref=info.at[other],
            dst_ref=info_out.at[me],
            send_sem=sems.at[0],
            recv_sem=sems.at[1],
            device_id=place(other),
            device_id_type=MESH,
        ).start()
        return carry

    lax.fori_loop(1, owners, tell, 0)
    info_out[me] = info[me]

    def matched_pair(other):
        first = other * CAP
        pair = jnp.concatenate([blocks[picks[first + j]] for j in range(CAP)], axis=0)
        coefs_of = [coefs[pl.ds(first + j, 1), :] for j in range(CAP)]
        totals = [jnp.zeros((rows, cols), jnp.float32) for _ in range(CAP)]
        step = 4
        for k in range(0, kinds, step):
            more = min(step, kinds - k)
            section = jnp.dot(
                pair,
                col_table[:, k * cols : (k + more) * cols],
                preferred_element_type=jnp.float32,
            ).astype(jnp.bfloat16)
            base = row_table[:, k * rows : (k + more) * rows]
            for j in range(CAP):
                stacked = jnp.concatenate(
                    [
                        section[j * rows : (j + 1) * rows, m * cols : (m + 1) * cols]
                        for m in range(more)
                    ],
                    axis=0,
                )
                coef = coefs_of[j][:, k * rows : (k + more) * rows]
                scaled = (coef * base).astype(jnp.bfloat16)
                totals[j] = totals[j] + jnp.dot(
                    scaled, stacked, preferred_element_type=jnp.float32
                )
        done = []
        for j in range(CAP):
            weight = coefs_of[j][:, kinds * rows : kinds * rows + 1]
            matched = totals[j].astype(jnp.bfloat16).astype(jnp.float32)
            done.append((weight * matched).astype(jnp.bfloat16))
        return jnp.concatenate(done, axis=0)

    def send(i, carry):
        other = lax.rem(me + i, owners)
        outgoing[other] = matched_pair(other)
        pltpu.make_async_remote_copy(
            src_ref=outgoing.at[other],
            dst_ref=pixels_out.at[me],
            send_sem=sems.at[2],
            recv_sem=sems.at[3],
            device_id=place(other),
            device_id_type=MESH,
        ).start()
        return carry

    lax.fori_loop(1, owners, send, 0)
    pixels_out[me] = matched_pair(me)
    others = pl.ds(0, owners - 1)
    for ref, pair in ((info, 0), (outgoing, 2)):
        for which in range(2):
            pltpu.make_async_copy(ref.at[others], ref.at[others], sems.at[pair + which]).wait()


def place_kernel(slots, rows, span_rows, span_cols, pixels, info, coadd, total):
    total[...] = jnp.zeros_like(total)
    cols = pixels.shape[2]
    lane = lax.broadcasted_iota(jnp.int32, (rows, cols), 1)

    def add(s, carry):
        row = span_rows[s]
        col = span_cols[s]
        tile = col // cols
        shift = col - tile * cols
        block = pltpu.roll(pixels[s].astype(jnp.float32), shift, 1)
        here = pl.ds(row, rows)
        left = lane >= shift
        total[tile, here, :] += jnp.where(left, block, 0.0)
        total[tile + 1, here, :] += jnp.where(left, 0.0, block)
        return carry

    lax.fori_loop(0, slots, add, 0)
    weight, top, left = info[:, 0:1], info[:, 1:2], info[:, 2:3]
    span = lax.broadcasted_iota(jnp.int32, (slots, PATCH), 1).astype(jnp.float32)
    row_weight = jnp.where((span >= top) & (span < top + rows), weight, 0.0).astype(jnp.bfloat16)
    col_cover = jnp.where((span >= left) & (span < left + cols), 1.0, 0.0).astype(jnp.bfloat16)
    depth = lax.dot_general(
        row_weight, col_cover, (((0,), (0,)), ((), ())), preferred_element_type=jnp.float32
    )
    value = jnp.concatenate([total[t] for t in range(PATCH // cols)], axis=1)
    coadd[...] = value / jnp.maximum(depth, 1.0)


def detect(coadd, det_taps):
    span = jnp.arange(PATCH)
    padded = padded_2(coadd, (("prow", 0), ("pcol", 1)), DET_R)
    wide = jnp.arange(PATCH + 2 * DET_R)
    reach = jnp.arange(2 * DET_R + 1)
    band_hits = (wide[None, :, None] - span[:, None, None] == reach[None, None, :]).astype(
        jnp.float32
    )
    band = jnp.sum(band_hits * det_taps[None, None, :], axis=2)
    across = jnp.dot(band, padded, precision=EXACT)
    return jnp.dot(across, band.T, precision=EXACT)


def shards(
    blocks,
    owner,
    row_offset,
    col_offset,
    exposure,
    basis_rows,
    basis_cols,
    coef_table,
    weight_table,
    det_taps,
):
    ncol = lax.axis_size("pcol")
    owners = lax.axis_size("prow") * ncol
    count, rows, cols = blocks.shape
    kinds, taps = basis_rows.shape
    entries = coef_table.shape[0]
    slots = owners * CAP
    vmem = pl.BlockSpec(memory_space=pltpu.VMEM)
    smem = pl.BlockSpec(memory_space=pltpu.SMEM)
    half = taps // 2

    feats = jnp.stack([row_offset, col_offset, jnp.arange(count, dtype=jnp.int32)], axis=1)
    feats = jnp.pad(feats.astype(jnp.float32), ((0, 0), (kinds + 1, LANES - kinds - 4)))
    table = jnp.concatenate([coef_table, weight_table[:, None]], axis=1)
    table = jnp.pad(table, ((0, 0), (0, LANES - kinds - 1)))
    flipped = jnp.pad(basis_cols.astype(jnp.float32)[:, ::-1], ((0, 0), (0, LANES - taps)))
    col_src = jnp.roll(flipped, -half, axis=1)
    narrow = jnp.pad(basis_rows.astype(jnp.float32), ((0, kinds % 2), (0, rows - taps)))
    row_src = jnp.roll(narrow.reshape(-1, 2 * rows), -half, axis=1)
    pairs = row_src.shape[0]

    info, coefs, col_table, row_table = pl.pallas_call(
        functools.partial(tables_kernel, kinds, slots),
        out_shape=(
            jax.ShapeDtypeStruct((slots, LANES), jnp.float32),
            jax.ShapeDtypeStruct((slots, (kinds + 1) * rows), jnp.float32),
            jax.ShapeDtypeStruct((cols, kinds * cols), jnp.bfloat16),
            jax.ShapeDtypeStruct((rows, pairs * 2 * rows), jnp.float32),
        ),
        in_specs=[vmem] * 7,
        out_specs=(vmem,) * 4,
        name="tables",
    )(owner, owner.reshape(1, count), feats, exposure[:, None], table, col_src, row_src)

    picks = info[:, kinds + 3].astype(jnp.int32)
    told = info[:, kinds : kinds + 3].reshape(owners, 1, CAP * 3)
    told = jnp.pad(told, ((0, 0), (0, 0), (0, LANES - CAP * 3)))
    pixels, heard = pl.pallas_call(
        functools.partial(route_kernel, owners, ncol, kinds),
        out_shape=(
            jax.ShapeDtypeStruct((owners, CAP * rows, cols), jnp.bfloat16),
            jax.ShapeDtypeStruct((owners, 1, LANES), jnp.float32),
        ),
        in_specs=[smem] + [vmem] * 5,
        out_specs=(vmem, vmem),
        scratch_shapes=[
            pltpu.VMEM((owners, CAP * rows, cols), jnp.bfloat16),
            pltpu.SemaphoreType.DMA((4,)),
        ],
        compiler_params=pltpu.CompilerParams(
            collective_id=0, has_side_effects=True, vmem_limit_bytes=48 * 1024 * 1024
        ),
        name="route",
    )(picks, blocks, coefs, told, col_table, row_table)

    told = heard[:, 0, : CAP * 3].reshape(slots, 3)
    spans = told[:, 1:].astype(jnp.int32)
    coadd = pl.pallas_call(
        functools.partial(place_kernel, slots, rows),
        out_shape=jax.ShapeDtypeStruct((PATCH, PATCH), jnp.float32),
        in_specs=[smem, smem, vmem, vmem],
        out_specs=vmem,
        scratch_shapes=[pltpu.VMEM((PATCH // cols + 1, PATCH, cols), jnp.float32)],
        compiler_params=pltpu.CompilerParams(vmem_limit_bytes=48 * 1024 * 1024),
        name="place",
    )(spans[:, 0], spans[:, 1], pixels.reshape(slots, rows, cols), told)
    return (coadd, detect(coadd, det_taps))


def solution(mesh):
    in_specs = (
        P(("prow", "pcol"), None, None),
        P(("prow", "pcol"), None),
        P(("prow", "pcol")),
        P(("prow", "pcol")),
        P(("prow", "pcol")),
        P(),
        P(),
        P(),
        P(),
        P(),
    )
    out_specs = (P("prow", "pcol"), P("prow", "pcol"))
    return jax.shard_map(shards, mesh=mesh, in_specs=in_specs, out_specs=out_specs, check_vma=False)
```

```python
import functools

import jax
import jax.numpy as jnp
from jax import lax
from jax.experimental import pallas as pl
from jax.experimental.pallas import tpu as pltpu
from jax.sharding import PartitionSpec as P

DET_R = 15
PATCH = 384
CAP = 2
LANES = 128
MESH = pl.DeviceIdType.MESH
EXACT = lax.Precision.HIGHEST


def prepare_kernel(kinds, owner, exposure, row_offset, col_offset, weights, coef_table, picks_out, told_out, coef_out):
    count = owner.shape[1]
    entries = weights.shape[1]
    slots = coef_out.shape[0]
    owners = slots // CAP
    at_sub = lax.broadcasted_iota(jnp.int32, (count, count), 0)
    at_lane = lax.broadcasted_iota(jnp.int32, (count, count), 1)

    def column(row):
        spread = jnp.broadcast_to(row, (count, count))
        return jnp.sum(jnp.where(at_sub == at_lane, spread, 0), axis=1, keepdims=True)

    same = jnp.where((column(owner[...]) == owner[...]) & (at_sub < at_lane), 1, 0)
    slot = owner[...] * CAP + jnp.sum(same, axis=0, keepdims=True)
    at_slot = lax.broadcasted_iota(jnp.int32, (count, slots), 1) == column(slot)
    numbers = lax.broadcasted_iota(jnp.int32, (count, slots), 0)
    picks_out[...] = jnp.sum(jnp.where(at_slot, numbers, 0), axis=0, keepdims=True)
    lane = lax.broadcasted_iota(jnp.int32, (owners, LANES), 1)
    told = jnp.zeros((owners, LANES), jnp.int32)
    for j in range(CAP):
        own = lax.broadcasted_iota(jnp.int32, (owners, count), 0) * CAP + j == slot
        values = (jnp.ones_like(slot), exposure[...], row_offset[...], col_offset[...])
        for n, value in enumerate(values):
            found = jnp.sum(jnp.where(own, value, 0), axis=1, keepdims=True)
            told = jnp.where(lane == 4 * j + n, found, told)
    for o in range(owners):
        told_out[o] = told[o : o + 1, :]
    own = lax.broadcasted_iota(jnp.int32, (slots, count), 0) == slot
    index = jnp.sum(jnp.where(own, exposure[...], 0), axis=1, keepdims=True)
    hits = lax.broadcasted_iota(jnp.int32, (slots, entries), 1) == index
    weight = jnp.sum(jnp.where(hits, weights[...], 0.0), axis=1, keepdims=True)
    weight = weight.astype(jnp.bfloat16).astype(jnp.float32)
    width = coef_out.shape[1]
    part = width // (kinds + 1)
    spread = (
        lax.broadcasted_iota(jnp.int32, (kinds, width), 0)
        == lax.broadcasted_iota(jnp.int32, (kinds, width), 1) // part
    ).astype(jnp.float32)
    coefs = lax.dot_general(
        hits.astype(jnp.float32),
        coef_table[...],
        (((1,), (1,)), ((), ())),
        precision=EXACT,
        preferred_element_type=jnp.float32,
    )
    coefs = jnp.dot(coefs, spread, precision=EXACT, preferred_element_type=jnp.float32)
    last = lax.broadcasted_iota(jnp.int32, (slots, width), 1) >= kinds * part
    coef_out[...] = jnp.where(last, weight, coefs)


def build_tables(basis_rows, basis_cols, col_out, row_out):
    kinds, taps = basis_rows.shape
    half = taps // 2
    rows, cols = row_out.shape[0], col_out.shape[0]
    tap = lax.broadcasted_iota(jnp.int32, (taps, LANES), 0)
    lane = lax.broadcasted_iota(jnp.int32, (taps, LANES), 1)

    def spread(value, target):
        hot = jnp.where(lane == (target + LANES) % LANES, 1.0, 0.0).astype(jnp.bfloat16)
        return jnp.dot(value[...], hot, preferred_element_type=jnp.float32)

    col_src = spread(basis_cols, half - tap)
    even = spread(basis_rows, tap - half)
    odd = spread(basis_rows, tap - half + rows)
    near = jnp.abs(
        lax.broadcasted_iota(jnp.int32, (cols, LANES), 1)
        - lax.broadcasted_iota(jnp.int32, (cols, LANES), 0)
    )
    for k in range(kinds):
        source = jnp.broadcast_to(col_src[k : k + 1, :], (cols, LANES))
        rolled = pltpu.roll(source, 0, 1, stride=1, stride_axis=0)
        col_out[:, k * LANES : (k + 1) * LANES] = jnp.where(near <= half, rolled, 0.0).astype(
            jnp.bfloat16
        )
    near = jnp.abs(
        lax.broadcasted_iota(jnp.int32, (rows, LANES), 1) % rows
        - lax.broadcasted_iota(jnp.int32, (rows, LANES), 0)
    )
    for k in range(0, kinds, 2):
        source = even[k : k + 1, :]
        if k + 1 < kinds:
            source = source + odd[k + 1 : k + 2, :]
        rolled = pltpu.roll(
            jnp.broadcast_to(source, (rows, LANES)), 0, 1, stride=1, stride_axis=0
        )
        row_out[:, k * rows : k * rows + LANES] = jnp.where(near <= half, rolled, 0.0)


def route_kernel(
    owners,
    ncol,
    kinds,
    picks,
    blocks,
    coefs,
    info,
    basis_rows,
    basis_cols,
    pixels_out,
    info_out,
    outgoing,
    col_table,
    row_table,
    sems,
):
    me = lax.axis_index("prow") * ncol + lax.axis_index("pcol")
    rows, cols = blocks.shape[1:]
    barrier = pltpu.get_barrier_semaphore()

    def place(device):
        return (device // ncol, device % ncol)

    def greet(i, carry):
        other = lax.rem(me + i, owners)
        pl.semaphore_signal(barrier, inc=1, device_id=place(other), device_id_type=MESH)
        return carry

    lax.fori_loop(1, owners, greet, 0)
    build_tables(basis_rows, basis_cols, col_table, row_table)
    pl.semaphore_wait(barrier, owners - 1)

    def tell(i, carry):
        other = lax.rem(me + i, owners)
        pltpu.make_async_remote_copy(
            src_ref=info.at[other],
            dst_ref=info_out.at[me],
            send_sem=sems.at[0],
            recv_sem=sems.at[1],
            device_id=place(other),
            device_id_type=MESH,
        ).start()
        return carry

    lax.fori_loop(1, owners, tell, 0)
    info_out[me] = info[me]

    group = 4
    step = 4

    def matched_group(first):
        slots_of = [
            lax.rem(first + n, owners) * CAP + j for n in range(group) for j in range(CAP)
        ]
        pixels = jnp.concatenate([blocks[picks[0, s]] for s in slots_of], axis=0)
        coefs_of = [coefs[pl.ds(s, 1), :] for s in slots_of]
        totals = [jnp.zeros((rows, cols), jnp.float32) for _ in slots_of]
        for k in range(0, kinds, step):
            more = min(step, kinds - k)
            section = jnp.dot(
                pixels,
                col_table[:, k * cols : (k + more) * cols],
                preferred_element_type=jnp.float32,
            ).astype(jnp.bfloat16)
            base = row_table[:, k * rows : (k + more) * rows]
            for j in range(len(slots_of)):
                stacked = jnp.concatenate(
                    [
                        section[j * rows : (j + 1) * rows, m * cols : (m + 1) * cols]
                        for m in range(more)
                    ],
                    axis=0,
                )
                coef = coefs_of[j][:, k * rows : (k + more) * rows]
                scaled = (coef * base).astype(jnp.bfloat16)
                totals[j] = totals[j] + jnp.dot(
                    scaled, stacked, preferred_element_type=jnp.float32
                )
        for n in range(group):
            for j in range(CAP):
                s = n * CAP + j
                weight = coefs_of[s][:, kinds * rows : kinds * rows + 1]
                matched = totals[s].astype(jnp.bfloat16).astype(jnp.float32)
                outgoing[lax.rem(first + n, owners), j * rows : (j + 1) * rows, :] = (
                    weight * matched
                ).astype(jnp.bfloat16)

    def send(g, carry):
        matched_group(me + g * group)
        for n in range(group):
            other = lax.rem(me + g * group + n, owners)

            @pl.when(g * group + n > 0)
            def _():
                pltpu.make_async_remote_copy(
                    src_ref=outgoing.at[other],
                    dst_ref=pixels_out.at[me],
                    send_sem=sems.at[2],
                    recv_sem=sems.at[3],
                    device_id=place(other),
                    device_id_type=MESH,
                ).start()

        return carry

    lax.fori_loop(0, owners // group, send, 0)
    pixels_out[me] = outgoing[me]
    others = pl.ds(0, owners - 1)
    for ref, pair in ((info, 0), (outgoing, 2)):
        for which in range(2):
            pltpu.make_async_copy(ref.at[others], ref.at[others], sems.at[pair + which]).wait()


def place_kernel(slots, rows, told, weights, pixels, coadd, total, row_weight, col_cover):
    total[...] = jnp.zeros_like(total)
    cols = pixels.shape[2]
    lane = lax.broadcasted_iota(jnp.int32, (rows, cols), 1)
    span = lax.broadcasted_iota(jnp.int32, (1, PATCH), 1)

    def add(o, carry):
        for j in range(CAP):
            s = o * CAP + j
            live = told[o, 0, 4 * j]
            exposure = told[o, 0, 4 * j + 1]
            row = told[o, 0, 4 * j + 2]
            col = told[o, 0, 4 * j + 3]
            tile = col // cols
            shift = col - tile * cols
            block = pltpu.roll(pixels[s].astype(jnp.float32), shift, 1)
            keep = jnp.where(live > 0, cols, 0)
            here = pl.ds(row, rows)
            left = lane >= shift
            total[tile, here, :] += jnp.where(left & (lane < keep), block, 0.0)
            total[tile + 1, here, :] += jnp.where(left | (lane >= keep), 0.0, block)
            weight = jnp.where(live > 0, weights[exposure], 0.0)
            row_weight[pl.ds(s, 1), :] = jnp.where((span >= row) & (span < row + rows), weight, 0.0)
            col_cover[pl.ds(s, 1), :] = jnp.where((span >= col) & (span < col + cols), 1.0, 0.0)
        return carry

    lax.fori_loop(0, slots // CAP, add, 0)
    depth = lax.dot_general(
        row_weight[...].astype(jnp.bfloat16),
        col_cover[...].astype(jnp.bfloat16),
        (((0,), (0,)), ((), ())),
        preferred_element_type=jnp.float32,
    )
    value = jnp.concatenate([total[t] for t in range(PATCH // cols)], axis=1)
    coadd[...] = value / jnp.maximum(depth, 1.0)


HALO = 16
WIDE = 512


def split_dot(left, right, dims):
    def parts(value):
        high = value.astype(jnp.bfloat16)
        return high, (value - high.astype(jnp.float32)).astype(jnp.bfloat16)

    (a, b), (c, d) = parts(left), parts(right)
    dot = functools.partial(
        lax.dot_general, dimension_numbers=(dims, ((), ())), preferred_element_type=jnp.float32
    )
    return dot(a, c) + (dot(a, d) + dot(b, c))


def detect_kernel(nrow, ncol, coadd, taps, detection, image, halo, sems):
    prow, pcol = lax.axis_index("prow"), lax.axis_index("pcol")
    top, bottom = pl.ds(0, HALO), pl.ds(PATCH - HALO, HALO)
    first, last, whole = pl.ds(0, LANES), pl.ds(PATCH - LANES, LANES), pl.ds(0, PATCH)
    left_tile, right_tile = pl.ds(PATCH, LANES), pl.ds(PATCH + LANES, LANES)
    below = pl.ds(HALO, HALO)
    moves = (
        (0, -1, image.at[below, whole], image.at[pl.ds(PATCH + HALO, HALO), whole]),
        (0, 1, image.at[pl.ds(PATCH, HALO), whole], image.at[top, whole]),
        (1, 0, coadd.at[bottom, whole], halo.at[top, whole]),
        (-1, 0, coadd.at[top, whole], halo.at[below, whole]),
        (1, 1, coadd.at[bottom, last], halo.at[top, left_tile]),
        (1, -1, coadd.at[bottom, first], halo.at[top, right_tile]),
        (-1, 1, coadd.at[top, last], halo.at[below, left_tile]),
        (-1, -1, coadd.at[top, first], halo.at[below, right_tile]),
    )

    def inside(dp, dc):
        row, col = prow + dp, pcol + dc
        return (row >= 0) & (row < nrow) & (col >= 0) & (col < ncol)

    halo[...] = jnp.zeros_like(halo)
    image[0:HALO, :] = jnp.zeros((HALO, WIDE), jnp.float32)
    image[PATCH + HALO :, :] = jnp.zeros((WIDE - PATCH - HALO, WIDE), jnp.float32)
    barrier = pltpu.get_barrier_semaphore()
    count = 0
    for dp, dc, _, _ in moves:
        count = count + jnp.where(inside(dp, dc), 1, 0)

        @pl.when(inside(dp, dc))
        def _():
            pl.semaphore_signal(
                barrier, inc=1, device_id=(prow + dp, pcol + dc), device_id_type=MESH
            )

    image[HALO : HALO + PATCH, 0:PATCH] = coadd[...].T
    pl.semaphore_wait(barrier, count)

    def copy(n):
        dp, dc, source, target = moves[n]
        return pltpu.make_async_remote_copy(
            src_ref=source,
            dst_ref=target,
            send_sem=sems.at[0, n],
            recv_sem=sems.at[1, n],
            device_id=(prow + dp, pcol + dc),
            device_id_type=MESH,
        )

    for n, (dp, dc, _, _) in enumerate(moves):

        @pl.when(inside(dp, dc))
        def _():
            copy(n).start()

    def band(shift):
        source = jnp.broadcast_to(taps[shift : shift + 1, :], (PATCH, WIDE))
        return pltpu.roll(source, 0, 1, stride=1, stride_axis=0)

    across = band(0)
    lane = lax.broadcasted_iota(jnp.int32, (PATCH, LANES), 1)
    edges = jnp.where(
        lane < HALO,
        across[:, 0:LANES],
        jnp.where(lane < 2 * HALO, across[:, PATCH:], 0.0),
    )
    down = jnp.concatenate([band(1)[:, 0:PATCH], edges], axis=1)

    for n, (dp, dc, _, _) in enumerate(moves):

        @pl.when(inside(dp, dc))
        def _():
            copy(n).wait_send()

        @pl.when(inside(-dp, -dc))
        def _():
            copy(n).wait_recv()

    turned = halo[...].T
    image[HALO : HALO + PATCH, PATCH:] = turned[0:PATCH, :]
    image[0:HALO, PATCH:] = turned[PATCH + LANES - HALO : PATCH + LANES, :]
    image[PATCH + HALO : PATCH + 2 * HALO, PATCH:] = turned[PATCH + LANES : PATCH + LANES + HALO, :]
    partial = split_dot(across, image[...], ((1,), (0,)))
    detection[...] = split_dot(down, partial, ((1,), (1,)))


def shards(
    blocks,
    owner,
    row_offset,
    col_offset,
    exposure,
    basis_rows,
    basis_cols,
    coef_table,
    weight_table,
    det_taps,
):
    nrow = lax.axis_size("prow")
    ncol = lax.axis_size("pcol")
    owners = nrow * ncol
    count, rows, cols = blocks.shape
    kinds, taps = basis_rows.shape
    slots = owners * CAP
    vmem = pl.BlockSpec(memory_space=pltpu.VMEM)
    smem = pl.BlockSpec(memory_space=pltpu.SMEM)

    picks, told, coefs = pl.pallas_call(
        functools.partial(prepare_kernel, kinds),
        out_shape=(
            jax.ShapeDtypeStruct((1, slots), jnp.int32),
            jax.ShapeDtypeStruct((owners, 1, LANES), jnp.int32),
            jax.ShapeDtypeStruct((slots, (kinds + 1) * rows), jnp.float32),
        ),
        in_specs=[vmem] * 6,
        out_specs=(vmem,) * 3,
        name="prepare",
    )(
        owner.reshape(1, count),
        exposure[None],
        row_offset[None],
        col_offset[None],
        weight_table[None],
        coef_table.T,
    )

    pixels, heard = pl.pallas_call(
        functools.partial(route_kernel, owners, ncol, kinds),
        out_shape=(
            jax.ShapeDtypeStruct((owners, CAP * rows, cols), jnp.bfloat16),
            jax.ShapeDtypeStruct((owners, 1, LANES), jnp.int32),
        ),
        in_specs=[smem] + [vmem] * 5,
        out_specs=(vmem, vmem),
        scratch_shapes=[
            pltpu.VMEM((owners, CAP * rows, cols), jnp.bfloat16),
            pltpu.VMEM((cols, kinds * cols), jnp.bfloat16),
            pltpu.VMEM((rows, (kinds + kinds % 2) * rows), jnp.float32),
            pltpu.SemaphoreType.DMA((4,)),
        ],
        compiler_params=pltpu.CompilerParams(
            collective_id=0, has_side_effects=True, vmem_limit_bytes=48 * 1024 * 1024
        ),
        name="route",
    )(picks, blocks, coefs, told, basis_rows, basis_cols)

    rounded = weight_table.astype(jnp.bfloat16).astype(jnp.float32)
    coadd = pl.pallas_call(
        functools.partial(place_kernel, slots, rows),
        out_shape=jax.ShapeDtypeStruct((PATCH, PATCH), jnp.float32),
        in_specs=[smem, smem, vmem],
        out_specs=vmem,
        scratch_shapes=[
            pltpu.VMEM((PATCH // cols + 1, PATCH, cols), jnp.float32),
            pltpu.VMEM((slots, PATCH), jnp.float32),
            pltpu.VMEM((slots, PATCH), jnp.float32),
        ],
        compiler_params=pltpu.CompilerParams(vmem_limit_bytes=48 * 1024 * 1024),
        name="place",
    )(heard, rounded, pixels.reshape(slots, rows, cols))

    reach = det_taps.shape[0]
    low = jnp.pad(det_taps, (1, WIDE - reach - 1))
    sources = jnp.stack([low, jnp.roll(low, -HALO)])
    detection = pl.pallas_call(
        functools.partial(detect_kernel, nrow, ncol),
        out_shape=jax.ShapeDtypeStruct((PATCH, PATCH), jnp.float32),
        in_specs=[vmem] * 2,
        out_specs=vmem,
        scratch_shapes=[
            pltpu.VMEM((WIDE, WIDE), jnp.float32),
            pltpu.VMEM((LANES, PATCH + 2 * LANES), jnp.float32),
            pltpu.SemaphoreType.DMA((2, 8)),
        ],
        compiler_params=pltpu.CompilerParams(
            collective_id=1, has_side_effects=True, vmem_limit_bytes=48 * 1024 * 1024
        ),
        name="detect",
    )(coadd, sources)
    return (coadd, detection)


def solution(mesh):
    in_specs = (
        P(("prow", "pcol"), None, None),
        P(("prow", "pcol"), None),
        P(("prow", "pcol")),
        P(("prow", "pcol")),
        P(("prow", "pcol")),
        P(),
        P(),
        P(),
        P(),
        P(),
    )
    out_specs = (P("prow", "pcol"), P("prow", "pcol"))
    return jax.shard_map(shards, mesh=mesh, in_specs=in_specs, out_specs=out_specs, check_vma=False)
```

```python
import functools

import jax
import jax.numpy as jnp
from jax import lax
from jax.experimental import pallas as pl
from jax.experimental.pallas import tpu as pltpu
from jax.sharding import PartitionSpec as P

DET_R = 15
PATCH = 384
CAP = 2
LANES = 128
MESH = pl.DeviceIdType.MESH
EXACT = lax.Precision.HIGHEST


HALO = 16
WIDE = 512


def split_dot(left, right, dims):
    def parts(value):
        high = value.astype(jnp.bfloat16)
        return high, (value - high.astype(jnp.float32)).astype(jnp.bfloat16)

    (a, b), (c, d) = parts(left), parts(right)
    dot = functools.partial(
        lax.dot_general, dimension_numbers=(dims, ((), ())), preferred_element_type=jnp.float32
    )
    return dot(a, c) + (dot(a, d) + dot(b, c))


def prepare(kinds, owner, exposure, row_offset, col_offset, weights, coef_table, picks_out, told_out, coef_out):
    count = owner.shape[1]
    entries = weights.shape[1]
    slots = coef_out.shape[0]
    owners = slots // CAP
    at_sub = lax.broadcasted_iota(jnp.int32, (count, count), 0)
    at_lane = lax.broadcasted_iota(jnp.int32, (count, count), 1)

    def column(row):
        spread = jnp.broadcast_to(row, (count, count))
        return jnp.sum(jnp.where(at_sub == at_lane, spread, 0), axis=1, keepdims=True)

    same = jnp.where((column(owner[...]) == owner[...]) & (at_sub < at_lane), 1, 0)
    slot = owner[...] * CAP + jnp.sum(same, axis=0, keepdims=True)
    at_slot = lax.broadcasted_iota(jnp.int32, (count, slots), 1) == column(slot)
    numbers = lax.broadcasted_iota(jnp.int32, (count, slots), 0)
    picks_out[...] = jnp.sum(jnp.where(at_slot, numbers, 0), axis=0, keepdims=True)
    lane = lax.broadcasted_iota(jnp.int32, (owners, LANES), 1)
    told = jnp.zeros((owners, LANES), jnp.int32)
    for j in range(CAP):
        own = lax.broadcasted_iota(jnp.int32, (owners, count), 0) * CAP + j == slot
        values = (jnp.ones_like(slot), exposure[...], row_offset[...], col_offset[...])
        for n, value in enumerate(values):
            found = jnp.sum(jnp.where(own, value, 0), axis=1, keepdims=True)
            told = jnp.where(lane == 4 * j + n, found, told)
    for o in range(owners):
        told_out[o] = told[o : o + 1, :]
    own = lax.broadcasted_iota(jnp.int32, (slots, count), 0) == slot
    index = jnp.sum(jnp.where(own, exposure[...], 0), axis=1, keepdims=True)
    hits = lax.broadcasted_iota(jnp.int32, (slots, entries), 1) == index
    weight = jnp.sum(jnp.where(hits, weights[...], 0.0), axis=1, keepdims=True)
    weight = weight.astype(jnp.bfloat16).astype(jnp.float32)
    width = coef_out.shape[1]
    part = width // (kinds + 1)
    spread = (
        lax.broadcasted_iota(jnp.int32, (kinds, width), 0)
        == lax.broadcasted_iota(jnp.int32, (kinds, width), 1) // part
    ).astype(jnp.float32)
    coefs = lax.dot_general(
        hits.astype(jnp.float32),
        coef_table[...],
        (((1,), (1,)), ((), ())),
        precision=EXACT,
        preferred_element_type=jnp.float32,
    )
    coefs = jnp.dot(coefs, spread, precision=EXACT, preferred_element_type=jnp.float32)
    last = lax.broadcasted_iota(jnp.int32, (slots, width), 1) >= kinds * part
    coef_out[...] = jnp.where(last, weight, coefs)


def build_tables(basis_rows, basis_cols, col_out, row_out):
    kinds, taps = basis_rows.shape
    half = taps // 2
    rows, cols = row_out.shape[0], col_out.shape[0]
    tap = lax.broadcasted_iota(jnp.int32, (taps, LANES), 0)
    lane = lax.broadcasted_iota(jnp.int32, (taps, LANES), 1)

    def spread(value, target):
        hot = jnp.where(lane == (target + LANES) % LANES, 1.0, 0.0).astype(jnp.bfloat16)
        return jnp.dot(value[...], hot, preferred_element_type=jnp.float32)

    col_src = spread(basis_cols, half - tap)
    even = spread(basis_rows, tap - half)
    odd = spread(basis_rows, tap - half + rows)
    near = jnp.abs(
        lax.broadcasted_iota(jnp.int32, (cols, LANES), 1)
        - lax.broadcasted_iota(jnp.int32, (cols, LANES), 0)
    )
    for k in range(kinds):
        source = jnp.broadcast_to(col_src[k : k + 1, :], (cols, LANES))
        rolled = pltpu.roll(source, 0, 1, stride=1, stride_axis=0)
        col_out[:, k * LANES : (k + 1) * LANES] = jnp.where(near <= half, rolled, 0.0).astype(
            jnp.bfloat16
        )
    near = jnp.abs(
        lax.broadcasted_iota(jnp.int32, (rows, LANES), 1) % rows
        - lax.broadcasted_iota(jnp.int32, (rows, LANES), 0)
    )
    for k in range(0, kinds, 2):
        source = even[k : k + 1, :]
        if k + 1 < kinds:
            source = source + odd[k + 1 : k + 2, :]
        rolled = pltpu.roll(
            jnp.broadcast_to(source, (rows, LANES)), 0, 1, stride=1, stride_axis=0
        )
        row_out[:, k * rows : k * rows + LANES] = jnp.where(near <= half, rolled, 0.0)


def whole_kernel(
    nrow,
    ncol,
    owner,
    exposure,
    row_offset,
    col_offset,
    weights,
    coef_table,
    basis_rows,
    basis_cols,
    taps,
    source_blocks,
    coadd,
    detection,
    blocks,
    pick_row,
    picks,
    info,
    coefs,
    col_table,
    row_table,
    outgoing,
    arrived,
    heard,
    total,
    image,
    halo,
    sems,
    data_sems,
    halo_sems,
):
    owners = nrow * ncol
    prow, pcol = lax.axis_index("prow"), lax.axis_index("pcol")
    me = prow * ncol + pcol
    rows, cols = blocks.shape[1:]
    kinds = basis_rows.shape[0]
    span = nrow // 2 if nrow % 2 == 0 else nrow

    def turn(i):
        step, col = i // ncol, (pcol + 1 + i) % ncol
        side = (prow // span + 1 + step // span) % (nrow // span)
        return (side * span + (prow + 1 + step) % span) * ncol + col

    def source(i):
        step, col = i // ncol, (pcol + 2 * ncol - 1 - i % ncol) % ncol
        side = (prow // span + 1 + step // span) % (nrow // span)
        return (side * span + (prow + 2 * span - 1 - step % span) % span) * ncol + col

    def place(device):
        return (device // ncol, device % ncol)

    load = pltpu.make_async_copy(source_blocks, blocks, sems.at[3])
    load.start()
    halo[...] = jnp.zeros_like(halo)
    image[0:HALO, :] = jnp.zeros((HALO, WIDE), jnp.float32)
    image[PATCH + HALO :, :] = jnp.zeros((WIDE - PATCH - HALO, WIDE), jnp.float32)
    barrier = pltpu.get_barrier_semaphore()

    def greet(i, carry):
        other = lax.rem(me + i, owners)
        pl.semaphore_signal(barrier, inc=1, device_id=place(other), device_id_type=MESH)
        return carry

    lax.fori_loop(1, owners, greet, 0)
    prepare(
        kinds, owner, exposure, row_offset, col_offset, weights, coef_table, pick_row, info, coefs
    )
    lift = pltpu.make_async_copy(pick_row, picks, sems.at[2])
    lift.start()
    build_tables(basis_rows, basis_cols, col_table, row_table)
    total[...] = jnp.zeros_like(total)
    lift.wait()
    load.wait()
    pl.semaphore_wait(barrier, owners - 1)

    def tell(i, carry):
        other = lax.rem(me + i, owners)
        pltpu.make_async_remote_copy(
            src_ref=info.at[other],
            dst_ref=heard.at[me],
            send_sem=sems.at[0],
            recv_sem=sems.at[1],
            device_id=place(other),
            device_id_type=MESH,
        ).start()
        return carry

    lax.fori_loop(1, owners, tell, 0)
    heard[me] = info[me]

    group = 2
    step = 4

    def matched_group(first):
        slots_of = [
            turn(first + n) * CAP + j for n in range(group) for j in range(CAP)
        ]
        pixels = jnp.concatenate([blocks[picks[0, s]] for s in slots_of], axis=0)
        coefs_of = [coefs[pl.ds(s, 1), :] for s in slots_of]
        totals = [jnp.zeros((rows, cols), jnp.float32) for _ in slots_of]
        for k in range(0, kinds, step):
            more = min(step, kinds - k)
            section = jnp.dot(
                pixels,
                col_table[:, k * cols : (k + more) * cols],
                preferred_element_type=jnp.float32,
            ).astype(jnp.bfloat16)
            base = row_table[:, k * rows : (k + more) * rows]
            for j in range(len(slots_of)):
                stacked = jnp.concatenate(
                    [
                        section[j * rows : (j + 1) * rows, m * cols : (m + 1) * cols]
                        for m in range(more)
                    ],
                    axis=0,
                )
                coef = coefs_of[j][:, k * rows : (k + more) * rows]
                scaled = (coef * base).astype(jnp.bfloat16)
                totals[j] = totals[j] + jnp.dot(
                    scaled, stacked, preferred_element_type=jnp.float32
                )
        for n in range(group):
            for j in range(CAP):
                s = n * CAP + j
                weight = coefs_of[s][:, kinds * rows : kinds * rows + 1]
                matched = totals[s].astype(jnp.bfloat16).astype(jnp.float32)
                outgoing[turn(first + n), j * rows : (j + 1) * rows, :] = (
                    weight * matched
                ).astype(jnp.bfloat16)

    def data_copy(other, origin):
        return pltpu.make_async_remote_copy(
            src_ref=outgoing.at[other],
            dst_ref=arrived.at[origin],
            send_sem=data_sems.at[0, other],
            recv_sem=data_sems.at[1, origin],
            device_id=place(other),
            device_id_type=MESH,
        )

    def send(g, carry):
        matched_group(g * group)
        for n in range(group):
            other = turn(g * group + n)

            @pl.when(g * group + n < owners - 1)
            def _():
                data_copy(other, me).start()

        return carry

    lax.fori_loop(0, owners // group, send, 0)
    arrived[me] = outgoing[me]
    others = pl.ds(0, owners - 1)
    for which in range(2):
        pltpu.make_async_copy(info.at[others], info.at[others], sems.at[which]).wait()

    wide = lax.broadcasted_iota(jnp.int32, (owners, PATCH), 1)
    entries = weights.shape[1]
    letters = jnp.concatenate([heard[o] for o in range(owners)], axis=0)
    depth = jnp.zeros((PATCH, PATCH), jnp.float32)
    for j in range(CAP):
        live, entry, top, left = (letters[:, 4 * j + n : 4 * j + n + 1] for n in range(4))
        hits = lax.broadcasted_iota(jnp.int32, (owners, entries), 1) == entry
        weight = jnp.sum(jnp.where(hits, weights[...], 0.0), axis=1, keepdims=True)
        weight = jnp.where(live > 0, weight, 0.0)
        row_weight = jnp.where((wide >= top) & (wide < top + rows), weight, 0.0)
        col_cover = jnp.where((wide >= left) & (wide < left + cols), 1.0, 0.0)
        depth = depth + lax.dot_general(
            row_weight.astype(jnp.bfloat16),
            col_cover.astype(jnp.bfloat16),
            (((0,), (0,)), ((), ())),
            preferred_element_type=jnp.float32,
        )
    coadd[...] = jnp.maximum(depth, 1.0)

    offset = lax.broadcasted_iota(jnp.int32, (cols, PATCH), 1) - lax.broadcasted_iota(
        jnp.int32, (cols, PATCH), 0
    )
    many = group * CAP
    down = lax.broadcasted_iota(jnp.int32, (PATCH, many * rows), 0)
    lane = lax.broadcasted_iota(jnp.int32, (1, many * rows), 1)

    def gather(g, carry):
        target = lane % rows
        shifted = []
        for n in range(group):
            origin = source(g * group + n)

            @pl.when(g * group + n < owners - 1)
            def _():
                data_copy(origin, origin).wait_recv()

            letter = heard[origin]
            for j in range(CAP):
                live, _, top, left = (letter[:, 4 * j + n : 4 * j + n + 1] for n in range(4))
                hot = jnp.where((offset == left) & (live > 0), 1.0, 0.0).astype(jnp.bfloat16)
                block = arrived[origin, j * rows : (j + 1) * rows, :]
                shifted.append(
                    jnp.dot(block, hot, preferred_element_type=jnp.float32).astype(jnp.bfloat16)
                )
                target = target + jnp.where(lane // rows == n * CAP + j, top, 0)
        hot = jnp.where(down == target, 1.0, 0.0).astype(jnp.bfloat16)
        total[...] += jnp.dot(
            hot, jnp.concatenate(shifted, axis=0), preferred_element_type=jnp.float32
        )
        return carry

    lax.fori_loop(0, owners // group, gather, 0)
    coadd[...] = total[...] / coadd[...]

    first_rows, last_rows = pl.ds(0, HALO), pl.ds(PATCH - HALO, HALO)
    first, last, whole = pl.ds(0, LANES), pl.ds(PATCH - LANES, LANES), pl.ds(0, PATCH)
    left_tile, right_tile = pl.ds(PATCH, LANES), pl.ds(PATCH + LANES, LANES)
    below = pl.ds(HALO, HALO)
    moves = (
        (1, 0, coadd.at[last_rows, whole], halo.at[first_rows, whole]),
        (-1, 0, coadd.at[first_rows, whole], halo.at[below, whole]),
        (1, 1, coadd.at[last_rows, last], halo.at[first_rows, left_tile]),
        (1, -1, coadd.at[last_rows, first], halo.at[first_rows, right_tile]),
        (-1, 1, coadd.at[first_rows, last], halo.at[below, left_tile]),
        (-1, -1, coadd.at[first_rows, first], halo.at[below, right_tile]),
        (0, -1, image.at[below, whole], image.at[pl.ds(PATCH + HALO, HALO), whole]),
        (0, 1, image.at[pl.ds(PATCH, HALO), whole], image.at[first_rows, whole]),
    )

    def inside(dp, dc):
        row, col = prow + dp, pcol + dc
        return (row >= 0) & (row < nrow) & (col >= 0) & (col < ncol)

    def halo_copy(n):
        dp, dc, origin, target = moves[n]
        return pltpu.make_async_remote_copy(
            src_ref=origin,
            dst_ref=target,
            send_sem=halo_sems.at[0, n],
            recv_sem=halo_sems.at[1, n],
            device_id=(prow + dp, pcol + dc),
            device_id_type=MESH,
        )

    for n, (dp, dc, _, _) in enumerate(moves):
        if dp == 0 and dc < 0:
            image[HALO : HALO + PATCH, 0:PATCH] = coadd[...].T

        @pl.when(inside(dp, dc))
        def _():
            halo_copy(n).start()

    def sent(i, carry):
        other = turn(i)
        data_copy(other, other).wait_send()
        return carry

    lax.fori_loop(0, owners - 1, sent, 0)

    def band(shift):
        origin = jnp.broadcast_to(taps[shift : shift + 1, :], (PATCH, WIDE))
        return pltpu.roll(origin, 0, 1, stride=1, stride_axis=0)

    across = band(0)
    lane = lax.broadcasted_iota(jnp.int32, (PATCH, LANES), 1)
    edges = jnp.where(
        lane < HALO,
        across[:, 0:LANES],
        jnp.where(lane < 2 * HALO, across[:, PATCH:], 0.0),
    )
    along = jnp.concatenate([band(1)[:, 0:PATCH], edges], axis=1)

    for n, (dp, dc, _, _) in enumerate(moves):

        @pl.when(inside(dp, dc))
        def _():
            halo_copy(n).wait_send()

        @pl.when(inside(-dp, -dc))
        def _():
            halo_copy(n).wait_recv()

    turned = halo[...].T
    image[HALO : HALO + PATCH, PATCH:] = turned[0:PATCH, :]
    image[0:HALO, PATCH:] = turned[PATCH + LANES - HALO : PATCH + LANES, :]
    image[PATCH + HALO : PATCH + 2 * HALO, PATCH:] = turned[PATCH + LANES : PATCH + LANES + HALO, :]
    partial = split_dot(across, image[...], ((1,), (0,)))
    detection[...] = split_dot(along, partial, ((1,), (1,)))


def shards(
    blocks,
    owner,
    row_offset,
    col_offset,
    exposure,
    basis_rows,
    basis_cols,
    coef_table,
    weight_table,
    det_taps,
):
    nrow = lax.axis_size("prow")
    ncol = lax.axis_size("pcol")
    owners = nrow * ncol
    count, rows, cols = blocks.shape
    kinds, taps = basis_rows.shape
    slots = owners * CAP
    vmem = pl.BlockSpec(memory_space=pltpu.VMEM)

    reach = det_taps.shape[0]
    low = jnp.pad(det_taps, (1, WIDE - reach - 1))
    bands = jnp.stack([low, jnp.roll(low, -HALO)])
    tract = jax.ShapeDtypeStruct((PATCH, PATCH), jnp.float32)
    even = kinds + kinds % 2
    return pl.pallas_call(
        functools.partial(whole_kernel, nrow, ncol),
        out_shape=(tract, tract),
        in_specs=[vmem] * 9 + [pl.BlockSpec(memory_space=pl.ANY)],
        out_specs=(vmem, vmem),
        scratch_shapes=[
            pltpu.VMEM((count, rows, cols), jnp.bfloat16),
            pltpu.VMEM((1, slots), jnp.int32),
            pltpu.SMEM((1, slots), jnp.int32),
            pltpu.VMEM((owners, 1, LANES), jnp.int32),
            pltpu.VMEM((slots, (kinds + 1) * rows), jnp.float32),
            pltpu.VMEM((cols, kinds * cols), jnp.bfloat16),
            pltpu.VMEM((rows, even * rows), jnp.float32),
            pltpu.VMEM((owners, CAP * rows, cols), jnp.bfloat16),
            pltpu.VMEM((owners, CAP * rows, cols), jnp.bfloat16),
            pltpu.VMEM((owners, 1, LANES), jnp.int32),
            pltpu.VMEM((PATCH, PATCH), jnp.float32),
            pltpu.VMEM((WIDE, WIDE), jnp.float32),
            pltpu.VMEM((LANES, PATCH + 2 * LANES), jnp.float32),
            pltpu.SemaphoreType.DMA((4,)),
            pltpu.SemaphoreType.DMA((2, owners)),
            pltpu.SemaphoreType.DMA((2, 8)),
        ],
        compiler_params=pltpu.CompilerParams(
            collective_id=0, has_side_effects=True, vmem_limit_bytes=56 * 1024 * 1024
        ),
        name="whole",
    )(
        owner.reshape(1, count),
        exposure[None],
        row_offset[None],
        col_offset[None],
        weight_table[None],
        coef_table.T,
        basis_rows,
        basis_cols,
        bands,
        blocks,
    )


def solution(mesh):
    in_specs = (
        P(("prow", "pcol"), None, None),
        P(("prow", "pcol"), None),
        P(("prow", "pcol")),
        P(("prow", "pcol")),
        P(("prow", "pcol")),
        P(),
        P(),
        P(),
        P(),
        P(),
    )
    out_specs = (P("prow", "pcol"), P("prow", "pcol"))
    return jax.shard_map(shards, mesh=mesh, in_specs=in_specs, out_specs=out_specs, check_vma=False)
```

```python
import functools

import jax
import jax.numpy as jnp
from jax import lax
from jax.experimental import pallas as pl
from jax.experimental.pallas import tpu as pltpu
from jax.sharding import PartitionSpec as P

DET_R = 15
PATCH = 384
CAP = 2
LANES = 128
MESH = pl.DeviceIdType.MESH
EXACT = lax.Precision.HIGHEST


HALO = 16
WIDE = 512


def split_dot(left, right, dims):
    def parts(value):
        high = value.astype(jnp.bfloat16)
        return high, (value - high.astype(jnp.float32)).astype(jnp.bfloat16)

    (a, b), (c, d) = parts(left), parts(right)
    dot = functools.partial(
        lax.dot_general, dimension_numbers=(dims, ((), ())), preferred_element_type=jnp.float32
    )
    return dot(a, c) + (dot(a, d) + dot(b, c))


def prepare(kinds, owner, exposure, row_offset, col_offset, weights, coef_table, picks_out, told_out, coef_out):
    count = owner.shape[1]
    entries = weights.shape[1]
    slots = coef_out.shape[0]
    owners = slots // CAP
    at_sub = lax.broadcasted_iota(jnp.int32, (count, count), 0)
    at_lane = lax.broadcasted_iota(jnp.int32, (count, count), 1)

    def column(row):
        spread = jnp.broadcast_to(row, (count, count))
        return jnp.sum(jnp.where(at_sub == at_lane, spread, 0), axis=1, keepdims=True)

    same = jnp.where((column(owner[...]) == owner[...]) & (at_sub < at_lane), 1, 0)
    slot = owner[...] * CAP + jnp.sum(same, axis=0, keepdims=True)
    at_slot = lax.broadcasted_iota(jnp.int32, (count, slots), 1) == column(slot)
    numbers = lax.broadcasted_iota(jnp.int32, (count, slots), 0)
    picks_out[...] = jnp.sum(jnp.where(at_slot, numbers, 0), axis=0, keepdims=True)
    lane = lax.broadcasted_iota(jnp.int32, (owners, LANES), 1)
    told = jnp.zeros((owners, LANES), jnp.int32)
    for j in range(CAP):
        own = lax.broadcasted_iota(jnp.int32, (owners, count), 0) * CAP + j == slot
        values = (jnp.ones_like(slot), exposure[...], row_offset[...], col_offset[...])
        for n, value in enumerate(values):
            found = jnp.sum(jnp.where(own, value, 0), axis=1, keepdims=True)
            told = jnp.where(lane == 4 * j + n, found, told)
    for o in range(owners):
        told_out[o] = told[o : o + 1, :]
    own = lax.broadcasted_iota(jnp.int32, (slots, count), 0) == slot
    index = jnp.sum(jnp.where(own, exposure[...], 0), axis=1, keepdims=True)
    hits = lax.broadcasted_iota(jnp.int32, (slots, entries), 1) == index
    weight = jnp.sum(jnp.where(hits, weights[...], 0.0), axis=1, keepdims=True)
    weight = weight.astype(jnp.bfloat16).astype(jnp.float32)
    width = coef_out.shape[1]
    part = width // (kinds + 1)
    spread = (
        lax.broadcasted_iota(jnp.int32, (kinds, width), 0)
        == lax.broadcasted_iota(jnp.int32, (kinds, width), 1) // part
    ).astype(jnp.float32)
    coefs = lax.dot_general(
        hits.astype(jnp.float32),
        coef_table[...],
        (((1,), (1,)), ((), ())),
        precision=EXACT,
        preferred_element_type=jnp.float32,
    )
    coefs = jnp.dot(coefs, spread, precision=EXACT, preferred_element_type=jnp.float32)
    last = lax.broadcasted_iota(jnp.int32, (slots, width), 1) >= kinds * part
    coef_out[...] = jnp.where(last, weight, coefs)


def build_tables(basis_rows, basis_cols, col_out, row_out):
    kinds, taps = basis_rows.shape
    half = taps // 2
    rows, cols = row_out.shape[0], col_out.shape[0]
    tap = lax.broadcasted_iota(jnp.int32, (taps, LANES), 0)
    lane = lax.broadcasted_iota(jnp.int32, (taps, LANES), 1)

    def spread(value, target):
        hot = jnp.where(lane == (target + LANES) % LANES, 1.0, 0.0).astype(jnp.bfloat16)
        return jnp.dot(value[...], hot, preferred_element_type=jnp.float32)

    col_src = spread(basis_cols, half - tap)
    even = spread(basis_rows, tap - half)
    odd = spread(basis_rows, tap - half + rows)
    near = jnp.abs(
        lax.broadcasted_iota(jnp.int32, (cols, LANES), 1)
        - lax.broadcasted_iota(jnp.int32, (cols, LANES), 0)
    )
    for k in range(kinds):
        source = jnp.broadcast_to(col_src[k : k + 1, :], (cols, LANES))
        rolled = pltpu.roll(source, 0, 1, stride=1, stride_axis=0)
        col_out[:, k * LANES : (k + 1) * LANES] = jnp.where(near <= half, rolled, 0.0).astype(
            jnp.bfloat16
        )
    near = jnp.abs(
        lax.broadcasted_iota(jnp.int32, (rows, LANES), 1) % rows
        - lax.broadcasted_iota(jnp.int32, (rows, LANES), 0)
    )
    for k in range(0, kinds, 2):
        source = even[k : k + 1, :]
        if k + 1 < kinds:
            source = source + odd[k + 1 : k + 2, :]
        rolled = pltpu.roll(
            jnp.broadcast_to(source, (rows, LANES)), 0, 1, stride=1, stride_axis=0
        )
        row_out[:, k * rows : k * rows + LANES] = jnp.where(near <= half, rolled, 0.0)


def whole_kernel(
    nrow,
    ncol,
    owner,
    exposure,
    row_offset,
    col_offset,
    weights,
    coef_table,
    basis_rows,
    basis_cols,
    taps,
    source_blocks,
    coadd,
    detection,
    blocks,
    pick_row,
    picks,
    info,
    coefs,
    col_table,
    row_table,
    outgoing,
    arrived,
    heard,
    total,
    image,
    halo,
    sems,
    data_sems,
    halo_sems,
):
    owners = nrow * ncol
    prow, pcol = lax.axis_index("prow"), lax.axis_index("pcol")
    me = prow * ncol + pcol
    rows, cols = blocks.shape[1:]
    kinds = basis_rows.shape[0]
    span = nrow // 2 if nrow % 2 == 0 else nrow

    def turn(i):
        step, col = i // ncol, (pcol + 1 + i) % ncol
        side = (prow // span + 1 + step // span) % (nrow // span)
        return (side * span + (prow + 1 + step) % span) * ncol + col

    def source(i):
        step, col = i // ncol, (pcol + 2 * ncol - 1 - i % ncol) % ncol
        side = (prow // span + 1 + step // span) % (nrow // span)
        return (side * span + (prow + 2 * span - 1 - step % span) % span) * ncol + col

    def place(device):
        return (device // ncol, device % ncol)

    load = pltpu.make_async_copy(source_blocks, blocks, sems.at[3])
    load.start()
    halo[...] = jnp.zeros_like(halo)
    image[0:HALO, :] = jnp.zeros((HALO, WIDE), jnp.float32)
    image[PATCH + HALO :, :] = jnp.zeros((WIDE - PATCH - HALO, WIDE), jnp.float32)
    barrier = pltpu.get_barrier_semaphore()

    def greet(i, carry):
        other = lax.rem(me + i, owners)
        pl.semaphore_signal(barrier, inc=1, device_id=place(other), device_id_type=MESH)
        return carry

    lax.fori_loop(1, owners, greet, 0)
    prepare(
        kinds, owner, exposure, row_offset, col_offset, weights, coef_table, pick_row, info, coefs
    )
    lift = pltpu.make_async_copy(pick_row, picks, sems.at[2])
    lift.start()
    build_tables(basis_rows, basis_cols, col_table, row_table)
    total[...] = jnp.zeros_like(total)
    lift.wait()
    load.wait()
    pl.semaphore_wait(barrier, owners - 1)

    def tell(i, carry):
        other = lax.rem(me + i, owners)
        pltpu.make_async_remote_copy(
            src_ref=info.at[other],
            dst_ref=heard.at[me],
            send_sem=sems.at[0],
            recv_sem=sems.at[1],
            device_id=place(other),
            device_id_type=MESH,
        ).start()
        return carry

    lax.fori_loop(1, owners, tell, 0)
    heard[me] = info[me]

    mgroup = 2
    step = 4

    def matched_group(first):
        slots_of = [
            turn(first + n) * CAP + j for n in range(mgroup) for j in range(CAP)
        ]
        pixels = jnp.concatenate([blocks[picks[0, s]] for s in slots_of], axis=0)
        coefs_of = [coefs[pl.ds(s, 1), :] for s in slots_of]
        totals = [jnp.zeros((rows, cols), jnp.float32) for _ in slots_of]
        for k in range(0, kinds, step):
            more = min(step, kinds - k)
            section = jnp.dot(
                pixels,
                col_table[:, k * cols : (k + more) * cols],
                preferred_element_type=jnp.float32,
            ).astype(jnp.bfloat16)
            base = row_table[:, k * rows : (k + more) * rows]
            for j in range(len(slots_of)):
                stacked = jnp.concatenate(
                    [
                        section[j * rows : (j + 1) * rows, m * cols : (m + 1) * cols]
                        for m in range(more)
                    ],
                    axis=0,
                )
                coef = coefs_of[j][:, k * rows : (k + more) * rows]
                scaled = (coef * base).astype(jnp.bfloat16)
                totals[j] = totals[j] + jnp.dot(
                    scaled, stacked, preferred_element_type=jnp.float32
                )
        for n in range(mgroup):
            for j in range(CAP):
                s = n * CAP + j
                weight = coefs_of[s][:, kinds * rows : kinds * rows + 1]
                matched = totals[s].astype(jnp.bfloat16).astype(jnp.float32)
                outgoing[turn(first + n), j * rows : (j + 1) * rows, :] = (
                    weight * matched
                ).astype(jnp.bfloat16)

    def data_copy(other, origin):
        return pltpu.make_async_remote_copy(
            src_ref=outgoing.at[other],
            dst_ref=arrived.at[origin],
            send_sem=data_sems.at[0, other],
            recv_sem=data_sems.at[1, origin],
            device_id=place(other),
            device_id_type=MESH,
        )

    def send(g, carry):
        matched_group(g * mgroup)
        for n in range(mgroup):
            other = turn(g * mgroup + n)

            @pl.when(g * mgroup + n < owners - 1)
            def _():
                data_copy(other, me).start()

        return carry

    lax.fori_loop(0, owners // mgroup, send, 0)
    arrived[me] = outgoing[me]
    others = pl.ds(0, owners - 1)
    for which in range(2):
        pltpu.make_async_copy(info.at[others], info.at[others], sems.at[which]).wait()

    wide = lax.broadcasted_iota(jnp.int32, (owners, PATCH), 1)
    entries = weights.shape[1]
    letters = jnp.concatenate([heard[o] for o in range(owners)], axis=0)
    depth = jnp.zeros((PATCH, PATCH), jnp.float32)
    for j in range(CAP):
        live, entry, top, left = (letters[:, 4 * j + n : 4 * j + n + 1] for n in range(4))
        hits = lax.broadcasted_iota(jnp.int32, (owners, entries), 1) == entry
        weight = jnp.sum(jnp.where(hits, weights[...], 0.0), axis=1, keepdims=True)
        weight = jnp.where(live > 0, weight, 0.0)
        row_weight = jnp.where((wide >= top) & (wide < top + rows), weight, 0.0)
        col_cover = jnp.where((wide >= left) & (wide < left + cols), 1.0, 0.0)
        depth = depth + lax.dot_general(
            row_weight.astype(jnp.bfloat16),
            col_cover.astype(jnp.bfloat16),
            (((0,), (0,)), ((), ())),
            preferred_element_type=jnp.float32,
        )
    coadd[...] = jnp.maximum(depth, 1.0)

    offset = lax.broadcasted_iota(jnp.int32, (cols, PATCH), 1) - lax.broadcasted_iota(
        jnp.int32, (cols, PATCH), 0
    )
    group = 4
    many = group * CAP
    down = lax.broadcasted_iota(jnp.int32, (PATCH, many * rows), 0)
    lane = lax.broadcasted_iota(jnp.int32, (1, many * rows), 1)

    def gather(g, carry):
        g = (g + owners // group // 2) % (owners // group)
        target = lane % rows
        shifted = []
        for n in range(group):
            origin = source(g * group + n)

            @pl.when(g * group + n < owners - 1)
            def _():
                data_copy(origin, origin).wait_recv()

            letter = heard[origin]
            for j in range(CAP):
                live, _, top, left = (letter[:, 4 * j + n : 4 * j + n + 1] for n in range(4))
                hot = jnp.where((offset == left) & (live > 0), 1.0, 0.0).astype(jnp.bfloat16)
                block = arrived[origin, j * rows : (j + 1) * rows, :]
                shifted.append(
                    jnp.dot(block, hot, preferred_element_type=jnp.float32).astype(jnp.bfloat16)
                )
                target = target + jnp.where(lane // rows == n * CAP + j, top, 0)
        hot = jnp.where(down == target, 1.0, 0.0).astype(jnp.bfloat16)
        total[...] += jnp.dot(
            hot, jnp.concatenate(shifted, axis=0), preferred_element_type=jnp.float32
        )
        return carry

    lax.fori_loop(0, owners // group, gather, 0)
    coadd[...] = total[...] / coadd[...]

    first_rows, last_rows = pl.ds(0, HALO), pl.ds(PATCH - HALO, HALO)
    first, last, whole = pl.ds(0, LANES), pl.ds(PATCH - LANES, LANES), pl.ds(0, PATCH)
    left_tile, right_tile = pl.ds(PATCH, LANES), pl.ds(PATCH + LANES, LANES)
    below = pl.ds(HALO, HALO)
    moves = (
        (1, 0, coadd.at[last_rows, whole], halo.at[first_rows, whole]),
        (-1, 0, coadd.at[first_rows, whole], halo.at[below, whole]),
        (1, 1, coadd.at[last_rows, last], halo.at[first_rows, left_tile]),
        (1, -1, coadd.at[last_rows, first], halo.at[first_rows, right_tile]),
        (-1, 1, coadd.at[first_rows, last], halo.at[below, left_tile]),
        (-1, -1, coadd.at[first_rows, first], halo.at[below, right_tile]),
        (0, -1, image.at[below, whole], image.at[pl.ds(PATCH + HALO, HALO), whole]),
        (0, 1, image.at[pl.ds(PATCH, HALO), whole], image.at[first_rows, whole]),
    )

    def inside(dp, dc):
        row, col = prow + dp, pcol + dc
        return (row >= 0) & (row < nrow) & (col >= 0) & (col < ncol)

    def halo_copy(n):
        dp, dc, origin, target = moves[n]
        return pltpu.make_async_remote_copy(
            src_ref=origin,
            dst_ref=target,
            send_sem=halo_sems.at[0, n],
            recv_sem=halo_sems.at[1, n],
            device_id=(prow + dp, pcol + dc),
            device_id_type=MESH,
        )

    for n, (dp, dc, _, _) in enumerate(moves):
        if dp == 0 and dc < 0:
            image[HALO : HALO + PATCH, 0:PATCH] = coadd[...].T

        @pl.when(inside(dp, dc))
        def _():
            halo_copy(n).start()

    def sent(i, carry):
        other = turn(i)
        data_copy(other, other).wait_send()
        return carry

    lax.fori_loop(0, owners - 1, sent, 0)

    def band(shift):
        origin = jnp.broadcast_to(taps[shift : shift + 1, :], (PATCH, WIDE))
        return pltpu.roll(origin, 0, 1, stride=1, stride_axis=0)

    across = band(0)
    lane = lax.broadcasted_iota(jnp.int32, (PATCH, LANES), 1)
    edges = jnp.where(
        lane < HALO,
        across[:, 0:LANES],
        jnp.where(lane < 2 * HALO, across[:, PATCH:], 0.0),
    )
    along = jnp.concatenate([band(1)[:, 0:PATCH], edges], axis=1)

    for n, (dp, dc, _, _) in enumerate(moves):

        @pl.when(inside(dp, dc))
        def _():
            halo_copy(n).wait_send()

        @pl.when(inside(-dp, -dc))
        def _():
            halo_copy(n).wait_recv()

    turned = halo[...].T
    image[HALO : HALO + PATCH, PATCH:] = turned[0:PATCH, :]
    image[0:HALO, PATCH:] = turned[PATCH + LANES - HALO : PATCH + LANES, :]
    image[PATCH + HALO : PATCH + 2 * HALO, PATCH:] = turned[PATCH + LANES : PATCH + LANES + HALO, :]
    partial = split_dot(across, image[...], ((1,), (0,)))
    detection[...] = split_dot(along, partial, ((1,), (1,)))


def shards(
    blocks,
    owner,
    row_offset,
    col_offset,
    exposure,
    basis_rows,
    basis_cols,
    coef_table,
    weight_table,
    det_taps,
):
    nrow = lax.axis_size("prow")
    ncol = lax.axis_size("pcol")
    owners = nrow * ncol
    count, rows, cols = blocks.shape
    kinds, taps = basis_rows.shape
    slots = owners * CAP
    vmem = pl.BlockSpec(memory_space=pltpu.VMEM)

    reach = det_taps.shape[0]
    low = jnp.pad(det_taps, (1, WIDE - reach - 1))
    bands = jnp.stack([low, jnp.roll(low, -HALO)])
    tract = jax.ShapeDtypeStruct((PATCH, PATCH), jnp.float32)
    even = kinds + kinds % 2
    return pl.pallas_call(
        functools.partial(whole_kernel, nrow, ncol),
        out_shape=(tract, tract),
        in_specs=[vmem] * 9 + [pl.BlockSpec(memory_space=pl.ANY)],
        out_specs=(vmem, vmem),
        scratch_shapes=[
            pltpu.VMEM((count, rows, cols), jnp.bfloat16),
            pltpu.VMEM((1, slots), jnp.int32),
            pltpu.SMEM((1, slots), jnp.int32),
            pltpu.VMEM((owners, 1, LANES), jnp.int32),
            pltpu.VMEM((slots, (kinds + 1) * rows), jnp.float32),
            pltpu.VMEM((cols, kinds * cols), jnp.bfloat16),
            pltpu.VMEM((rows, even * rows), jnp.float32),
            pltpu.VMEM((owners, CAP * rows, cols), jnp.bfloat16),
            pltpu.VMEM((owners, CAP * rows, cols), jnp.bfloat16),
            pltpu.VMEM((owners, 1, LANES), jnp.int32),
            pltpu.VMEM((PATCH, PATCH), jnp.float32),
            pltpu.VMEM((WIDE, WIDE), jnp.float32),
            pltpu.VMEM((LANES, PATCH + 2 * LANES), jnp.float32),
            pltpu.SemaphoreType.DMA((4,)),
            pltpu.SemaphoreType.DMA((2, owners)),
            pltpu.SemaphoreType.DMA((2, 8)),
        ],
        compiler_params=pltpu.CompilerParams(
            collective_id=0, has_side_effects=True, vmem_limit_bytes=56 * 1024 * 1024
        ),
        name="whole",
    )(
        owner.reshape(1, count),
        exposure[None],
        row_offset[None],
        col_offset[None],
        weight_table[None],
        coef_table.T,
        basis_rows,
        basis_cols,
        bands,
        blocks,
    )


def solution(mesh):
    in_specs = (
        P(("prow", "pcol"), None, None),
        P(("prow", "pcol"), None),
        P(("prow", "pcol")),
        P(("prow", "pcol")),
        P(("prow", "pcol")),
        P(),
        P(),
        P(),
        P(),
        P(),
    )
    out_specs = (P("prow", "pcol"), P("prow", "pcol"))
    return jax.shard_map(shards, mesh=mesh, in_specs=in_specs, out_specs=out_specs, check_vma=False)
```
